32 devices in a mesh: parts: 2 (over x), chain: 4 (over z), tile: 4 (over y, core).
Axes of the slice: x: 2, y: 2, z: 4, core: 2. Of those that a mesh axis runs over, the one named last changes fastest.
Arguments:
- leaf_rhs: float32 [8, 64, 128, 512], P(('parts', 'chain'), 'tile'), parts along dimension 0, may hold values from -6 to 6
- leaf_inverse: float32 [8, 64, 128, 128], P(('parts', 'chain'), 'tile'), parts along dimension 0, may hold values from -1 to 2, as said below
- leaf_coupling: float32 [8, 64, 128, 128], P(('parts', 'chain'), 'tile'), parts along dimension 0, may hold values from -0.5 to 0.5
- leaf_update: float32 [8, 64, 128, 128], P(('parts', 'chain'), 'tile'), parts along dimension 0, may hold values from -0.0625 to 0.0625
- update_pattern: int32 [8, 64], P(('parts', 'chain'), 'tile'), parts along dimension 0, may hold values 0 or 1
- sep_rhs: float32 [8, 128, 512], P(('parts', 'chain')), parts along dimension 0, may hold values from -6 to 6
- sep_inverse: float32 [8, 128, 128], P(('parts', 'chain')), parts along dimension 0, may hold values from -1 to 2, as said below
- sep_coupling: float32 [8, 128, 128], P(('parts', 'chain')), parts along dimension 0, may hold values from -0.5 to 0.5
Outputs:
- leaf_solution: float32 [8, 64, 128, 512], P(('parts', 'chain'), 'tile'), parts along dimension 0
- sep_solution: float32 [8, 128, 512], P(('parts', 'chain'), None, 'tile'), parts along dimension 0
The draws below stay inside these ranges and needn't reach their ends.
There are 2 independent parts, one for each index of `parts`. The reference program is written for one: setup_inputs(seed, part) draws one part's arguments, and reference() takes and returns one part's arrays. A program takes and returns all parts, laid end to end along the dimension named above; each array names one. Nothing has to cross between parts.
Inputs may be any that keep to these rules, and one draw needn't show every extreme that they name: `leaf_inverse`: each tile is lower triangular with a diagonal between 0.3 and 2. `sep_inverse`: each tile is lower triangular with a positive diagonal.
All inputs are finite; a program needn't handle non-finite values. No bound on the sum of `update_pattern` on one device may be relied on, other than what follows from the above.
Results may differ from the reference program's by a relative error of at most 0.00017.
Values sent between devices are 32-bit elements; how exact they have to be, the bound alone decides.
No kernel may reach another device: no remote copies, remote signals or barrier semaphores. Data moves between devices by JAX's collectives and lax.ppermute only.
A program may use at most 64 MiB of HBM per device.

```python
import jax
import jax.numpy as jnp
from jax import lax

TILE = 128
RHS = 512
LEAVES = 64
SECTIONS = 4


def lower_tiles(noise, diag_key, lead, diag_low, diag_high, spread):
    rows_index = lax.broadcasted_iota(jnp.int32, (TILE, TILE), 0)
    cols_index = lax.broadcasted_iota(jnp.int32, (TILE, TILE), 1)
    diagonal = jnp.exp(jax.random.uniform(diag_key, lead + (TILE,), jnp.float32, jnp.log(diag_low), jnp.log(diag_high)))
    below = jnp.clip(noise * (spread / jnp.sqrt(jnp.float32(TILE))), -1.0, 1.0)
    lower = jnp.where(rows_index > cols_index, below, 0.0)
    return lower + jnp.where(rows_index == cols_index, diagonal[..., None], 0.0)


def draw_leaf_inverse(key, part):
    noise_key, diag_key = jax.random.split(jax.random.fold_in(key, 11))
    shape = (SECTIONS, LEAVES, TILE, TILE)
    noise = jax.random.normal(noise_key, shape, jnp.float32)
    return lower_tiles(noise, diag_key, (SECTIONS, LEAVES), 0.5, 2.0, 0.5)


def draw_sep_inverse(key, part):
    noise_key, diag_key = jax.random.split(jax.random.fold_in(key, 23))
    shape = (SECTIONS, TILE, TILE)
    noise = jax.random.normal(noise_key, shape, jnp.float32)
    return lower_tiles(noise, diag_key, (SECTIONS,), 0.3, 0.9, 0.3)


def place_ends(result, stream_key, low, largest):
    longest = result.shape.index(max(result.shape))
    spots = []
    for shift in (0, 1):
        where = [jax.random.randint(jax.random.fold_in(stream_key, axis), (), 0, length) for axis, length in enumerate(result.shape)]
        where[longest] = (where[longest] + shift) % result.shape[longest]
        spots.append(tuple(where))
    return result.at[spots[0]].set(low).at[spots[1]].set(largest)


def block_levels(key, shape, cuts, smallest, top_value):
    level = 1.0
    for dim, parts in cuts:
        steps = jax.random.uniform(jax.random.fold_in(jax.random.fold_in(key, 6), dim), (parts,), jnp.float32, smallest / len(cuts), top_value / len(cuts))
        level = level * jnp.repeat(jnp.exp(steps), shape[dim] // parts).reshape((-1,) + (1,) * (len(shape) - 1 - dim))
    return level


def scatter_about(own_key, shape, deviation, most, pieces=(), held_as=jnp.bfloat16):
    gain = block_levels(own_key, shape, pieces, -0.22, 0.18) if pieces else 1.0
    array = jax.random.normal(own_key, shape, jnp.float32) * deviation * gain
    return jnp.minimum(jnp.maximum(array, -most), most).astype(held_as)


def setup_inputs(seed: int = 0, part: int = 0) -> dict:
    splits = jax.random.split(jax.random.key(seed), 9)
    own_keys = jax.random.split(jax.random.fold_in(splits[8], part), 9)
    leaf_rhs = scatter_about(own_keys[0], (SECTIONS, LEAVES, TILE, RHS), 1.0, 6.0, ((0, 4), (1, 4)), jnp.float32)
    leaf_inverse = draw_leaf_inverse(jax.random.fold_in(jax.random.fold_in(splits[8], part), 71), part)
    leaf_coupling = scatter_about(own_keys[2], (SECTIONS, LEAVES, TILE, TILE), TILE ** -0.5, 0.5, ((0, 4), (1, 4)), jnp.float32)
    leaf_update = scatter_about(own_keys[3], (SECTIONS, LEAVES, TILE, TILE), (TILE * LEAVES) ** -0.5, 0.0625, ((0, 4), (1, 4)), jnp.float32)
    update_pattern = place_ends((jax.random.randint(own_keys[4], (SECTIONS, LEAVES), 0, 4) < 3).astype(jnp.int32), jax.random.fold_in(own_keys[4], 1), 0, 1)
    sep_rhs = scatter_about(own_keys[5], (SECTIONS, TILE, RHS), 1.0, 6.0, ((0, 4),), jnp.float32)
    sep_inverse = draw_sep_inverse(jax.random.fold_in(jax.random.fold_in(splits[8], part), 71), part)
    sep_coupling = scatter_about(own_keys[7], (SECTIONS, TILE, TILE), TILE ** -0.5, 0.5, ((0, 4),), jnp.float32)
    return {"leaf_rhs": leaf_rhs, "leaf_inverse": leaf_inverse, "leaf_coupling": leaf_coupling, "leaf_update": leaf_update, "update_pattern": update_pattern, "sep_rhs": sep_rhs, "sep_inverse": sep_inverse, "sep_coupling": sep_coupling}


def reference(leaf_rhs, leaf_inverse, leaf_coupling, leaf_update, update_pattern, sep_rhs, sep_inverse, sep_coupling):
    highest = lax.Precision.HIGHEST
    carry_in = jnp.zeros((TILE, RHS), jnp.float32)
    leaf_parts = []
    sep_parts = []
    for section in range(SECTIONS):
        reduced = leaf_rhs[section] - jnp.einsum("lij,jr->lir", leaf_coupling[section], carry_in, precision=highest)
        leaf_values = jnp.einsum("lij,ljr->lir", leaf_inverse[section], reduced, precision=highest)
        pattern_mask = update_pattern[section].astype(jnp.float32)
        masked_update = leaf_update[section] * pattern_mask[:, None, None]
        update_sum = jnp.einsum("lij,ljr->ir", masked_update, leaf_values, precision=highest)
        inner = sep_rhs[section] - jnp.dot(sep_coupling[section], carry_in, precision=highest) - update_sum
        sep_values = jnp.dot(sep_inverse[section], inner, precision=highest)
        leaf_parts.append(leaf_values)
        sep_parts.append(sep_values)
        carry_in = sep_values
    return jnp.stack(leaf_parts), jnp.stack(sep_parts)
```

```python
import jax
import jax.numpy as jnp
from jax import lax
from jax.sharding import PartitionSpec as P

PRECISION = lax.Precision.HIGH


def swapped(block, axis, bit):
    route = [(i, i ^ bit) for i in range(lax.axis_size(axis))]
    return lax.ppermute(block, axis, route)


def product(left, right):
    return jnp.dot(left, right, precision=PRECISION)


def shards(
    leaf_rhs,
    leaf_inverse,
    leaf_coupling,
    leaf_update,
    update_pattern,
    sep_rhs,
    sep_inverse,
    sep_coupling,
):
    tiles = lax.axis_size("tile")
    sections = lax.axis_size("chain")
    tile = lax.axis_index("tile")
    section = lax.axis_index("chain")
    core = tile % 2
    rows, columns = sep_rhs.shape[1:]
    half = columns // 2
    width = columns // tiles

    def of_core(block, which):
        split = block.reshape(rows, tiles // 2, 2, width)
        return jnp.where(which == 0, split[:, :, 0], split[:, :, 1]).reshape(rows, half)

    inverse_tiles = leaf_inverse[0]
    solved_free = jnp.einsum("lij,ljr->lir", inverse_tiles, leaf_rhs[0], precision=PRECISION)
    gain_tiles = jnp.einsum("lij,ljk->lik", inverse_tiles, leaf_coupling[0], precision=PRECISION)
    masked_update = leaf_update[0] * update_pattern[0].astype(jnp.float32)[:, None, None]
    local_sum = jnp.einsum("lij,ljr->ir", masked_update, solved_free, precision=PRECISION)
    local_cross = jnp.einsum("lij,ljk->ik", masked_update, gain_tiles, precision=PRECISION)

    total = jnp.concatenate([of_core(local_sum, core), local_cross], 1)
    total = total + swapped(jnp.concatenate([of_core(local_sum, 1 - core), local_cross], 1), "tile", 1)
    bit = 2
    while bit < tiles:
        total = total + swapped(total, "tile", bit)
        bit *= 2
    right = jnp.concatenate([of_core(sep_rhs[0], core), sep_coupling[0]], 1)
    solved = product(sep_inverse[0], right - total)
    offset, step_map = solved[:, :half], -solved[:, half:]

    whole_b, whole_a = offset, step_map
    before_b, before_a = jnp.zeros_like(offset), jnp.eye(rows, dtype=offset.dtype)
    bit = 1
    while bit < sections:
        last = 2 * bit >= sections
        upper = (section // bit) % 2 == 1
        if last:
            other_b = swapped(whole_b, "chain", bit)
        else:
            other = swapped(jnp.concatenate([whole_b, whole_a], 1), "chain", bit)
            other_b, other_a = other[:, :half], other[:, half:]
        if bit == 1:
            stepped = other_b
        else:
            stepped = before_b + product(before_a, other_b)
        before_b = jnp.where(upper, stepped, before_b)
        if not last:
            if bit == 1:
                stepped = other_a
            else:
                stepped = product(before_a, other_a)
            before_a = jnp.where(upper, stepped, before_a)
            first_b = jnp.where(upper, other_b, whole_b)
            first_a = jnp.where(upper, other_a, whole_a)
            second_b = jnp.where(upper, whole_b, other_b)
            second_a = jnp.where(upper, whole_a, other_a)
            whole_b = second_b + product(second_a, first_b)
            if 4 * bit < sections:
                whole_a = product(second_a, first_a)
        bit *= 2
    carry_half = before_b

    sep_half = product(step_map, carry_half) + offset
    sep_share = lax.dynamic_slice_in_dim(sep_half, (tile // 2) * width, width, 1)
    other_half = swapped(carry_half, "tile", 1)
    pieces = [h.reshape(rows, tiles // 2, 1, width) for h in (carry_half, other_half)]
    carry = jnp.where(core == 0, jnp.concatenate(pieces, 2), jnp.concatenate(pieces[::-1], 2))
    carry = carry.reshape(rows, columns)
    leaf_values = solved_free - jnp.einsum("lik,kr->lir", gain_tiles, carry, precision=PRECISION)
    return (leaf_values[None], sep_share[None])


def solution(mesh):
    return jax.shard_map(
        shards,
        mesh=mesh,
        in_specs=(
            P(("parts", "chain"), "tile", None, None),
            P(("parts", "chain"), "tile", None, None),
            P(("parts", "chain"), "tile", None, None),
            P(("parts", "chain"), "tile", None, None),
            P(("parts", "chain"), "tile"),
            P(("parts", "chain"), None, None),
            P(("parts", "chain"), None, None),
            P(("parts", "chain"), None, None),
        ),
        out_specs=(P(("parts", "chain"), "tile", None, None), P(("parts", "chain"), None, "tile")),
        check_vma=False,
    )
```

```python
import functools

import jax
import jax.numpy as jnp
from jax import lax
from jax.experimental import pallas as pl
from jax.experimental.pallas import tpu as pltpu
from jax.sharding import PartitionSpec as P

F32 = jnp.float32
BF16 = jnp.bfloat16
LANES = 128
VMEM = pltpu.MemorySpace.VMEM
IN_VMEM = pl.BlockSpec(memory_space=pltpu.VMEM)
IN_HBM = pl.BlockSpec(memory_space=pl.ANY)
GROUP = 4


def swapped(block, axis, bit):
    route = [(i, i ^ bit) for i in range(lax.axis_size(axis))]
    return lax.ppermute(block, axis, route)


def parts_of(block):
    high = block.astype(BF16)
    return high, (block - high.astype(F32)).astype(BF16)


def matmul(left, right):
    return lax.dot_general(left, right, (((1,), (0,)), ((), ())), preferred_element_type=F32)


def left_of(block):
    high, low = parts_of(block)
    return jnp.concatenate([high, low, high], 1)


def right_of(block):
    high, low = parts_of(block)
    return jnp.concatenate([high, high, low], 0)


def product(left, right):
    return matmul(left_of(left), right_of(right))


def starts(tiles, which):
    if tiles == 4:
        return [which * LANES, which * LANES + 2 * LANES]
    return [which * 2 * LANES, which * 2 * LANES + LANES]


def lanes(start):
    return pl.ds(pl.multiple_of(start, LANES), LANES)


def reduce_kernel(tiles, pattern, rhs, inverse, coupling, update, sent, kept, highs, lows, inverses, right, tiles_a, tiles_b, sems):
    leaves = rhs.shape[0]
    rows = rhs.shape[1]
    core = lax.rem(lax.axis_index("tile"), 2)
    order = starts(tiles, 1 - core) + starts(tiles, core)
    copies = []
    for k in range(leaves // GROUP):
        some = pl.ds(k * GROUP, GROUP)
        pair = [
            pltpu.make_async_copy(update.at[some], tiles_a.at[some], sems.at[k, 0]),
            pltpu.make_async_copy(inverse.at[some], tiles_b.at[some], sems.at[k, 1]),
        ]
        for copy in pair:
            copy.start()
        copies.append(pair)
    blocks = []
    for k in range(leaves // GROUP):
        some = pl.ds(k * GROUP, GROUP)
        row = []
        for j, start in enumerate(order):
            place = j * LANES if j < 2 else (j + 1) * LANES
            row.append(pltpu.make_async_copy(rhs.at[some, :, lanes(start)], right.at[some, :, pl.ds(place, LANES)], sems.at[k, 2 + j]))
        row.append(pltpu.make_async_copy(coupling.at[some], right.at[some, :, pl.ds(2 * LANES, LANES)], sems.at[k, 6]))
        for copy in row:
            copy.start()
        blocks.append(row)
    lefts = []
    for k in range(leaves // GROUP):
        for copy in copies[k]:
            copy.wait()
        for leaf in range(k * GROUP, k * GROUP + GROUP):
            inv_high, inv_low = parts_of(tiles_b[leaf])
            inverses[leaf] = jnp.concatenate([inv_high, inv_low, inv_high], 1)
            masked = tiles_a[leaf] * pattern[0, leaf].astype(F32)
            lefts.append(left_of(matmul(left_of(masked), jnp.concatenate([inv_high, inv_high, inv_low], 0))))
    total = None
    for k in range(leaves // GROUP):
        for copy in blocks[k]:
            copy.wait()
        stacked = []
        for leaf in range(k * GROUP, k * GROUP + GROUP):
            high, low = parts_of(right[leaf])
            highs[leaf] = high
            lows[leaf] = low
            stacked += [high, high, low]
        here = matmul(jnp.concatenate(lefts[k * GROUP : k * GROUP + GROUP], 1), jnp.concatenate(stacked, 0))
        total = here if total is None else total + here
    sent[...] = total[:, : 3 * LANES]
    kept[:, : 2 * LANES] = total[:, 3 * LANES :]
    kept[:, 2 * LANES :] = total[:, 2 * LANES : 3 * LANES]


def reduced(tiles, pattern, rhs, inverse, coupling, update):
    leaves, rows, columns = rhs.shape
    wide = columns + rows
    return pl.pallas_call(
        functools.partial(reduce_kernel, tiles),
        out_shape=(
            VMEM((rows, columns // 2 + rows), F32),
            VMEM((rows, columns // 2 + rows), F32),
            VMEM((leaves, rows, wide), BF16),
            VMEM((leaves, rows, wide), BF16),
            VMEM((leaves, rows, 3 * rows), BF16),
        ),
        in_specs=[pl.BlockSpec(memory_space=pltpu.SMEM)] + [IN_HBM] * 4,
        out_specs=(IN_VMEM,) * 5,
        scratch_shapes=[
            pltpu.VMEM((leaves, rows, wide), F32),
            pltpu.VMEM((leaves, rows, rows), F32),
            pltpu.VMEM((leaves, rows, rows), F32),
            pltpu.SemaphoreType.DMA((leaves // GROUP, 7)),
        ],
        compiler_params=pltpu.CompilerParams(vmem_limit_bytes=50 << 20),
    )(pattern, rhs, inverse, coupling, update)


def free_kernel(highs, lows, inverses, solved, gains):
    for leaf in range(highs.shape[0]):
        high = highs[leaf]
        here = matmul(inverses[leaf], jnp.concatenate([high, high, lows[leaf]], 0))
        solved[leaf, :, : 2 * LANES] = here[:, : 2 * LANES]
        solved[leaf, :, 2 * LANES :] = here[:, 3 * LANES :]
        gains[leaf] = left_of(here[:, 2 * LANES : 3 * LANES])


def freed(highs, lows, inverses):
    leaves, rows, wide = highs.shape
    columns = wide - rows
    return pl.pallas_call(
        free_kernel,
        out_shape=(VMEM((leaves, rows, columns), F32), VMEM((leaves, rows, 3 * rows), BF16)),
        in_specs=[IN_VMEM] * 3,
        out_specs=(IN_VMEM,) * 2,
        compiler_params=pltpu.CompilerParams(vmem_limit_bytes=20 << 20),
        cost_estimate=pl.CostEstimate(flops=6 * leaves * rows * rows * wide, bytes_accessed=leaves * rows * wide * 8, transcendentals=0),
    )(highs, lows, inverses)


def section_kernel(tiles, received, kept, sep_rhs, sep_inverse, sep_coupling, solved):
    core = lax.rem(lax.axis_index("tile"), 2)
    first, second = starts(tiles, core)
    right = jnp.concatenate([sep_rhs[:, lanes(first)], sep_rhs[:, lanes(second)], sep_coupling[...]], 1)
    solved[...] = product(sep_inverse[...], right - (received[...] + kept[...]))


def section_map(tiles, received, kept, sep_rhs, sep_inverse, sep_coupling):
    return pl.pallas_call(
        functools.partial(section_kernel, tiles),
        out_shape=VMEM(kept.shape, F32),
        in_specs=[IN_VMEM] * 5,
        out_specs=IN_VMEM,
    )(received, kept, sep_rhs, sep_inverse, sep_coupling)


def pair_kernel(mine, other, whole):
    half = whole.shape[1]

    @pl.when(lax.rem(lax.axis_index("chain"), 2) == 1)
    def _():
        whole[...] = mine[:, :half] - product(mine[:, half:], other[:, :half])

    @pl.when(lax.rem(lax.axis_index("chain"), 2) == 0)
    def _():
        whole[...] = other[:, :half] - product(other[:, half:], mine[:, :half])


def paired(mine, other, half):
    return pl.pallas_call(
        pair_kernel,
        out_shape=VMEM((mine.shape[0], half), F32),
        in_specs=[IN_VMEM] * 2,
        out_specs=IN_VMEM,
    )(mine, other)


def carry_kernel(other, received, carry):
    half = carry.shape[1]
    section = lax.axis_index("chain")

    @pl.when(section == 0)
    def _():
        carry[...] = jnp.zeros_like(carry)

    @pl.when(section == 1)
    def _():
        carry[...] = other[:, :half]

    @pl.when(section == 2)
    def _():
        carry[...] = received[...]

    @pl.when(section == 3)
    def _():
        carry[...] = other[:, :half] - product(other[:, half:], received[...])


def carried(other, received):
    return pl.pallas_call(
        carry_kernel,
        out_shape=VMEM(received.shape, F32),
        in_specs=[IN_VMEM] * 2,
        out_specs=IN_VMEM,
    )(other, received)


def affine_kernel(step, block, offset, result):
    result[...] = offset[...] - product(step[...], block[...])


def affine(step, block, offset):
    return pl.pallas_call(
        affine_kernel,
        out_shape=VMEM(offset.shape, F32),
        in_specs=[IN_VMEM] * 3,
        out_specs=IN_VMEM,
    )(step, block, offset)


def scanned(section, solved, half):
    sections = lax.axis_size("chain")
    whole_b, whole_a = solved[:, :half], solved[:, half:]
    before_b, before_a = jnp.zeros_like(whole_b), -jnp.eye(whole_a.shape[0], dtype=F32)
    nothing = jnp.zeros_like(whole_a)
    bit = 1
    while bit < sections:
        upper = (section // bit) % 2 == 1
        other = swapped(jnp.concatenate([whole_b, whole_a], 1), "chain", bit)
        other_b, other_a = other[:, :half], other[:, half:]
        before_b = jnp.where(upper, affine(before_a, other_b, before_b), before_b)
        before_a = jnp.where(upper, affine(before_a, other_a, nothing), before_a)
        first_b, first_a = jnp.where(upper, other_b, whole_b), jnp.where(upper, other_a, whole_a)
        second_b, second_a = jnp.where(upper, whole_b, other_b), jnp.where(upper, whole_a, other_a)
        whole_b = affine(second_a, first_b, second_b)
        whole_a = affine(second_a, first_a, nothing)
        bit *= 2
    return before_b


def last_kernel(tiles, solved, gains, theirs, mine, out, values, sems):
    leaves = solved.shape[0]
    core = lax.rem(lax.axis_index("tile"), 2)
    order = starts(tiles, 1 - core) + starts(tiles, core)
    right = jnp.concatenate([right_of(theirs[...]), right_of(mine[...])], 1)
    copies = []
    for k in range(leaves // GROUP):
        for leaf in range(k * GROUP, k * GROUP + GROUP):
            values[leaf] = solved[leaf] - matmul(gains[leaf], right)
        some = pl.ds(k * GROUP, GROUP)
        for j, start in enumerate(order):
            copy = pltpu.make_async_copy(values.at[some, :, pl.ds(j * LANES, LANES)], out.at[some, :, lanes(start)], sems.at[k, j])
            copy.start()
            copies.append(copy)
    for copy in copies:
        copy.wait()


def leaf_values(tiles, solved, gains, theirs, mine):
    return pl.pallas_call(
        functools.partial(last_kernel, tiles),
        out_shape=jax.ShapeDtypeStruct(solved.shape, F32),
        in_specs=[IN_VMEM] * 4,
        out_specs=IN_HBM,
        scratch_shapes=[pltpu.VMEM(solved.shape, F32), pltpu.SemaphoreType.DMA((solved.shape[0] // GROUP, 4))],
        compiler_params=pltpu.CompilerParams(vmem_limit_bytes=20 << 20),
    )(solved, gains, theirs, mine)


def shards(
    leaf_rhs,
    leaf_inverse,
    leaf_coupling,
    leaf_update,
    update_pattern,
    sep_rhs,
    sep_inverse,
    sep_coupling,
):
    tiles = lax.axis_size("tile")
    sections = lax.axis_size("chain")
    tile = lax.axis_index("tile")
    section = lax.axis_index("chain")
    columns = sep_rhs.shape[2]
    half = columns // 2
    width = columns // tiles

    sent, kept, highs, lows, inverses = reduced(tiles, update_pattern, leaf_rhs[0], leaf_inverse[0], leaf_coupling[0], leaf_update[0])
    kept = kept + swapped(sent, "tile", 1)
    received = swapped(kept, "tile", 2) if tiles > 2 else jnp.zeros_like(kept)
    bit = 4
    while bit < tiles:
        kept = kept + received
        received = swapped(kept, "tile", bit)
        bit *= 2
    solved, gains = freed(highs, lows, inverses)
    mapped = section_map(tiles, received, kept, sep_rhs[0], sep_inverse[0], sep_coupling[0])
    if sections == 4:
        other = swapped(mapped, "chain", 1)
        whole = paired(mapped, other, half)
        carry = carried(other, swapped(whole, "chain", 2))
    else:
        carry = scanned(section, mapped, half)
    theirs = swapped(carry, "tile", 1)
    sep_values = affine(mapped[:, half:], carry, mapped[:, :half])
    if tiles == 4:
        sep_share = lax.dynamic_slice_in_dim(sep_values, (tile // 2) * width, width, 1)
    else:
        other_values = swapped(sep_values, "tile", 1)
        lower = jnp.where(tile % 2 == 0, sep_values, other_values)
        upper = jnp.where(tile % 2 == 0, other_values, sep_values)
        sep_share = lax.dynamic_slice_in_dim(jnp.concatenate([lower, upper], 1), tile * width, width, 1)
    return (leaf_values(tiles, solved, gains, theirs, carry)[None], sep_share[None])


def solution(mesh):
    return jax.shard_map(
        shards,
        mesh=mesh,
        in_specs=(
            P(("parts", "chain"), "tile", None, None),
            P(("parts", "chain"), "tile", None, None),
            P(("parts", "chain"), "tile", None, None),
            P(("parts", "chain"), "tile", None, None),
            P(("parts", "chain"), "tile"),
            P(("parts", "chain"), None, None),
            P(("parts", "chain"), None, None),
            P(("parts", "chain"), None, None),
        ),
        out_specs=(P(("parts", "chain"), "tile", None, None), P(("parts", "chain"), None, "tile")),
        check_vma=False,
    )
```

```python
import functools

import jax
import jax.numpy as jnp
from jax import lax
from jax.experimental import pallas as pl
from jax.experimental.pallas import tpu as pltpu
from jax.sharding import PartitionSpec as P

F32 = jnp.float32
BF16 = jnp.bfloat16
LANES = 128
VMEM = pltpu.MemorySpace.VMEM
IN_VMEM = pl.BlockSpec(memory_space=pltpu.VMEM)
IN_HBM = pl.BlockSpec(memory_space=pl.ANY)
GROUP = 4
SMALL = 4 << 20


def swapped(block, axis, bit):
    route = [(i, i ^ bit) for i in range(lax.axis_size(axis))]
    return lax.ppermute(block, axis, route)


def parts_of(block):
    high = block.astype(BF16)
    return high, (block - high.astype(F32)).astype(BF16)


def matmul(left, right):
    return lax.dot_general(left, right, (((1,), (0,)), ((), ())), preferred_element_type=F32)


def left_of(block):
    high, low = parts_of(block)
    return jnp.concatenate([high, low, high], 1)


def right_of(block):
    high, low = parts_of(block)
    return jnp.concatenate([high, high, low], 0)


def product(left, right):
    return matmul(left_of(left), right_of(right))


def starts(tiles, which):
    if tiles == 4:
        return [which * LANES, which * LANES + 2 * LANES]
    return [which * 2 * LANES, which * 2 * LANES + LANES]


def lanes(start):
    return pl.ds(pl.multiple_of(start, LANES), LANES)


def reduce_kernel(tiles, pattern, rhs, inverse, coupling, update, sent, kept, highs, lows, inverses, right, tiles_a, tiles_b, sems):
    leaves = rhs.shape[0]
    rows = rhs.shape[1]
    core = lax.rem(lax.axis_index("tile"), 2)
    order = starts(tiles, 1 - core) + starts(tiles, core)
    copies = []
    for k in range(leaves // GROUP):
        some = pl.ds(k * GROUP, GROUP)
        pair = [
            pltpu.make_async_copy(update.at[some], tiles_a.at[some], sems.at[k, 0]),
            pltpu.make_async_copy(inverse.at[some], tiles_b.at[some], sems.at[k, 1]),
        ]
        for copy in pair:
            copy.start()
        copies.append(pair)
    blocks = []
    for k in range(leaves // GROUP):
        some = pl.ds(k * GROUP, GROUP)
        row = []
        for j, start in enumerate(order):
            place = j * LANES if j < 2 else (j + 1) * LANES
            row.append(pltpu.make_async_copy(rhs.at[some, :, lanes(start)], right.at[some, :, pl.ds(place, LANES)], sems.at[k, 2 + j]))
        row.append(pltpu.make_async_copy(coupling.at[some], right.at[some, :, pl.ds(2 * LANES, LANES)], sems.at[k, 6]))
        for copy in row:
            copy.start()
        blocks.append(row)
    lefts = []
    for k in range(leaves // GROUP):
        for copy in copies[k]:
            copy.wait()
        for leaf in range(k * GROUP, k * GROUP + GROUP):
            inv_high, inv_low = parts_of(tiles_b[leaf])
            inverses[leaf] = jnp.concatenate([inv_high, inv_low, inv_high], 1)
            masked = tiles_a[leaf] * pattern[0, leaf].astype(F32)
            lefts.append(left_of(matmul(left_of(masked), jnp.concatenate([inv_high, inv_high, inv_low], 0))))
    total = None
    for k in range(leaves // GROUP):
        for copy in blocks[k]:
            copy.wait()
        stacked = []
        for leaf in range(k * GROUP, k * GROUP + GROUP):
            high, low = parts_of(right[leaf])
            highs[leaf] = high
            lows[leaf] = low
            stacked += [high, high, low]
        here = matmul(jnp.concatenate(lefts[k * GROUP : k * GROUP + GROUP], 1), jnp.concatenate(stacked, 0))
        total = here if total is None else total + here
    sent[...] = total[:, : 3 * LANES]
    kept[:, : 2 * LANES] = total[:, 3 * LANES :]
    kept[:, 2 * LANES :] = total[:, 2 * LANES : 3 * LANES]


def reduced(tiles, pattern, rhs, inverse, coupling, update):
    leaves, rows, columns = rhs.shape
    wide = columns + rows
    return pl.pallas_call(
        functools.partial(reduce_kernel, tiles),
        out_shape=(
            VMEM((rows, columns // 2 + rows), F32),
            VMEM((rows, columns // 2 + rows), F32),
            VMEM((leaves, rows, wide), BF16),
            VMEM((leaves, rows, wide), BF16),
            VMEM((leaves, rows, 3 * rows), BF16),
        ),
        in_specs=[pl.BlockSpec(memory_space=pltpu.SMEM)] + [IN_HBM] * 4,
        out_specs=(IN_VMEM,) * 5,
        scratch_shapes=[
            pltpu.VMEM((leaves, rows, wide), F32),
            pltpu.VMEM((leaves, rows, rows), F32),
            pltpu.VMEM((leaves, rows, rows), F32),
            pltpu.SemaphoreType.DMA((leaves // GROUP, 7)),
        ],
        compiler_params=pltpu.CompilerParams(vmem_limit_bytes=50 << 20),
    )(pattern, rhs, inverse, coupling, update)


def free_kernel(highs, lows, inverses, solved, gains):
    for leaf in range(highs.shape[0]):
        high = highs[leaf]
        here = matmul(inverses[leaf], jnp.concatenate([high, high, lows[leaf]], 0))
        solved[leaf, :, : 2 * LANES] = here[:, : 2 * LANES]
        solved[leaf, :, 2 * LANES :] = here[:, 3 * LANES :]
        gains[leaf] = left_of(here[:, 2 * LANES : 3 * LANES])


def freed(highs, lows, inverses):
    leaves, rows, wide = highs.shape
    columns = wide - rows
    return pl.pallas_call(
        free_kernel,
        out_shape=(VMEM((leaves, rows, columns), F32), VMEM((leaves, rows, 3 * rows), BF16)),
        in_specs=[IN_VMEM] * 3,
        out_specs=(IN_VMEM,) * 2,
        compiler_params=pltpu.CompilerParams(vmem_limit_bytes=12 << 20),
        cost_estimate=pl.CostEstimate(flops=6 * leaves * rows * rows * wide, bytes_accessed=leaves * rows * wide * 8, transcendentals=0),
    )(highs, lows, inverses)


def section_kernel(tiles, received, kept, sep_rhs, sep_inverse, sep_coupling, solved):
    core = lax.rem(lax.axis_index("tile"), 2)
    first, second = starts(tiles, core)
    right = jnp.concatenate([sep_rhs[:, lanes(first)], sep_rhs[:, lanes(second)], sep_coupling[...]], 1)
    solved[...] = product(sep_inverse[...], right - (received[...] + kept[...]))


def section_map(tiles, received, kept, sep_rhs, sep_inverse, sep_coupling):
    return pl.pallas_call(
        functools.partial(section_kernel, tiles),
        out_shape=VMEM(kept.shape, F32),
        in_specs=[IN_VMEM] * 5,
        out_specs=IN_VMEM,
        compiler_params=pltpu.CompilerParams(vmem_limit_bytes=SMALL),
    )(received, kept, sep_rhs, sep_inverse, sep_coupling)


def pair_kernel(mine, other, whole):
    half = whole.shape[1]

    @pl.when(lax.rem(lax.axis_index("chain"), 2) == 1)
    def _():
        whole[...] = mine[:, :half] - product(mine[:, half:], other[:, :half])

    @pl.when(lax.rem(lax.axis_index("chain"), 2) == 0)
    def _():
        whole[...] = other[:, :half] - product(other[:, half:], mine[:, :half])


def paired(mine, other, half):
    return pl.pallas_call(
        pair_kernel,
        out_shape=VMEM((mine.shape[0], half), F32),
        in_specs=[IN_VMEM] * 2,
        out_specs=IN_VMEM,
        compiler_params=pltpu.CompilerParams(vmem_limit_bytes=SMALL),
    )(mine, other)


def carry_kernel(other, received, carry):
    half = carry.shape[1]
    section = lax.axis_index("chain")

    @pl.when(section == 0)
    def _():
        carry[...] = jnp.zeros_like(carry)

    @pl.when(section == 1)
    def _():
        carry[...] = other[:, :half]

    @pl.when(section == 2)
    def _():
        carry[...] = received[...]

    @pl.when(section == 3)
    def _():
        carry[...] = other[:, :half] - product(other[:, half:], received[...])


def carried(other, received):
    return pl.pallas_call(
        carry_kernel,
        out_shape=VMEM(received.shape, F32),
        in_specs=[IN_VMEM] * 2,
        out_specs=IN_VMEM,
        compiler_params=pltpu.CompilerParams(vmem_limit_bytes=SMALL),
    )(other, received)


def affine_kernel(step, block, offset, result):
    result[...] = offset[...] - product(step[...], block[...])


def affine(step, block, offset):
    return pl.pallas_call(
        affine_kernel,
        out_shape=VMEM(offset.shape, F32),
        in_specs=[IN_VMEM] * 3,
        out_specs=IN_VMEM,
        compiler_params=pltpu.CompilerParams(vmem_limit_bytes=SMALL),
    )(step, block, offset)


def scanned(section, solved, half):
    sections = lax.axis_size("chain")
    whole_b, whole_a = solved[:, :half], solved[:, half:]
    before_b, before_a = jnp.zeros_like(whole_b), -jnp.eye(whole_a.shape[0], dtype=F32)
    nothing = jnp.zeros_like(whole_a)
    bit = 1
    while bit < sections:
        upper = (section // bit) % 2 == 1
        other = swapped(jnp.concatenate([whole_b, whole_a], 1), "chain", bit)
        other_b, other_a = other[:, :half], other[:, half:]
        before_b = jnp.where(upper, affine(before_a, other_b, before_b), before_b)
        before_a = jnp.where(upper, affine(before_a, other_a, nothing), before_a)
        first_b, first_a = jnp.where(upper, other_b, whole_b), jnp.where(upper, other_a, whole_a)
        second_b, second_a = jnp.where(upper, whole_b, other_b), jnp.where(upper, whole_a, other_a)
        whole_b = affine(second_a, first_b, second_b)
        whole_a = affine(second_a, first_a, nothing)
        bit *= 2
    return before_b


def last_kernel(tiles, solved, gains, theirs, mine, out, values, sems):
    leaves = solved.shape[0]
    core = lax.rem(lax.axis_index("tile"), 2)
    order = starts(tiles, 1 - core) + starts(tiles, core)
    right = jnp.concatenate([right_of(theirs[...]), right_of(mine[...])], 1)
    copies = []
    for k in range(leaves // GROUP):
        for leaf in range(k * GROUP, k * GROUP + GROUP):
            values[leaf] = solved[leaf] - matmul(gains[leaf], right)
        some = pl.ds(k * GROUP, GROUP)
        for j, start in enumerate(order):
            copy = pltpu.make_async_copy(values.at[some, :, pl.ds(j * LANES, LANES)], out.at[some, :, lanes(start)], sems.at[k, j])
            copy.start()
            copies.append(copy)
    for copy in copies:
        copy.wait()


def leaf_values(tiles, solved, gains, theirs, mine):
    return pl.pallas_call(
        functools.partial(last_kernel, tiles),
        out_shape=jax.ShapeDtypeStruct(solved.shape, F32),
        in_specs=[IN_VMEM] * 4,
        out_specs=IN_HBM,
        scratch_shapes=[pltpu.VMEM(solved.shape, F32), pltpu.SemaphoreType.DMA((solved.shape[0] // GROUP, 4))],
        compiler_params=pltpu.CompilerParams(vmem_limit_bytes=12 << 20),
    )(solved, gains, theirs, mine)


def shards(
    leaf_rhs,
    leaf_inverse,
    leaf_coupling,
    leaf_update,
    update_pattern,
    sep_rhs,
    sep_inverse,
    sep_coupling,
):
    tiles = lax.axis_size("tile")
    sections = lax.axis_size("chain")
    tile = lax.axis_index("tile")
    section = lax.axis_index("chain")
    columns = sep_rhs.shape[2]
    half = columns // 2
    width = columns // tiles

    sent, kept, highs, lows, inverses = reduced(tiles, update_pattern, leaf_rhs[0], leaf_inverse[0], leaf_coupling[0], leaf_update[0])
    kept = kept + swapped(sent, "tile", 1)
    received = swapped(kept, "tile", 2) if tiles > 2 else jnp.zeros_like(kept)
    bit = 4
    while bit < tiles:
        kept = kept + received
        received = swapped(kept, "tile", bit)
        bit *= 2
    solved, gains = freed(highs, lows, inverses)
    received, solved, gains = lax.optimization_barrier((received, solved, gains))
    mapped = section_map(tiles, received, kept, sep_rhs[0], sep_inverse[0], sep_coupling[0])
    if sections == 4:
        other = swapped(mapped, "chain", 1)
        whole = paired(mapped, other, half)
        carry = carried(other, swapped(whole, "chain", 2))
    else:
        carry = scanned(section, mapped, half)
    theirs = swapped(carry, "tile", 1)
    sep_values = affine(mapped[:, half:], carry, mapped[:, :half])
    if tiles == 4:
        sep_share = lax.dynamic_slice_in_dim(sep_values, (tile // 2) * width, width, 1)
    else:
        other_values = swapped(sep_values, "tile", 1)
        lower = jnp.where(tile % 2 == 0, sep_values, other_values)
        upper = jnp.where(tile % 2 == 0, other_values, sep_values)
        sep_share = lax.dynamic_slice_in_dim(jnp.concatenate([lower, upper], 1), tile * width, width, 1)
    return (leaf_values(tiles, solved, gains, theirs, carry)[None], sep_share[None])


def solution(mesh):
    return jax.shard_map(
        shards,
        mesh=mesh,
        in_specs=(
            P(("parts", "chain"), "tile", None, None),
            P(("parts", "chain"), "tile", None, None),
            P(("parts", "chain"), "tile", None, None),
            P(("parts", "chain"), "tile", None, None),
            P(("parts", "chain"), "tile"),
            P(("parts", "chain"), None, None),
            P(("parts", "chain"), None, None),
            P(("parts", "chain"), None, None),
        ),
        out_specs=(P(("parts", "chain"), "tile", None, None), P(("parts", "chain"), None, "tile")),
        check_vma=False,
    )
```

```python
import functools

import jax
import jax.numpy as jnp
from jax import lax
from jax.experimental import pallas as pl
from jax.experimental.pallas import tpu as pltpu
from jax.sharding import PartitionSpec as P

F32 = jnp.float32
BF16 = jnp.bfloat16
LANES = 128
VMEM = pltpu.MemorySpace.VMEM
IN_VMEM = pl.BlockSpec(memory_space=pltpu.VMEM)
IN_HBM = pl.BlockSpec(memory_space=pl.ANY)
GROUP = 4
SMALL = 4 << 20


def swapped(block, axis, bit):
    route = [(i, i ^ bit) for i in range(lax.axis_size(axis))]
    return lax.ppermute(block, axis, route)


def parts_of(block):
    high = block.astype(BF16)
    return high, (block - high.astype(F32)).astype(BF16)


def matmul(left, right):
    return lax.dot_general(left, right, (((1,), (0,)), ((), ())), preferred_element_type=F32)


def left_of(block):
    high, low = parts_of(block)
    return jnp.concatenate([high, low, high], 1)


def right_of(block):
    high, low = parts_of(block)
    return jnp.concatenate([high, high, low], 0)


def product(left, right):
    return matmul(left_of(left), right_of(right))


def starts(tiles, which):
    if tiles == 4:
        return [which * LANES, which * LANES + 2 * LANES]
    return [which * 2 * LANES, which * 2 * LANES + LANES]


def lanes(start):
    return pl.ds(pl.multiple_of(start, LANES), LANES)


def reduce_kernel(tiles, pattern, rhs, inverse, coupling, update, sent_a, kept_a, sent_b, kept_b, highs, lows, inverses, right, tiles_a, tiles_b, sems):
    leaves = rhs.shape[0]
    core = lax.rem(lax.axis_index("tile"), 2)
    other, own = starts(tiles, 1 - core), starts(tiles, core)
    order = [other[0], own[0], other[1], own[1]]
    copies = []
    for k in range(leaves // GROUP):
        some = pl.ds(k * GROUP, GROUP)
        pair = [
            pltpu.make_async_copy(update.at[some], tiles_a.at[some], sems.at[k, 0]),
            pltpu.make_async_copy(inverse.at[some], tiles_b.at[some], sems.at[k, 1]),
        ]
        for copy in pair:
            copy.start()
        copies.append(pair)
    blocks = []
    for k in range(leaves // GROUP):
        some = pl.ds(k * GROUP, GROUP)
        row = [pltpu.make_async_copy(coupling.at[some], right.at[some, :, pl.ds(0, LANES)], sems.at[k, 6])]
        for j, start in enumerate(order):
            row.append(pltpu.make_async_copy(rhs.at[some, :, lanes(start)], right.at[some, :, pl.ds((j + 1) * LANES, LANES)], sems.at[k, 2 + j]))
        for copy in row:
            copy.start()
        blocks.append(row)
    lefts = []
    for k in range(leaves // GROUP):
        for copy in copies[k]:
            copy.wait()
        for leaf in range(k * GROUP, k * GROUP + GROUP):
            inv_high, inv_low = parts_of(tiles_b[leaf])
            inverses[leaf] = jnp.concatenate([inv_high, inv_low, inv_high], 1)
            masked = tiles_a[leaf] * pattern[0, leaf].astype(F32)
            lefts.append(left_of(matmul(left_of(masked), jnp.concatenate([inv_high, inv_high, inv_low], 0))))
    total = None
    for k in range(leaves // GROUP):
        for copy in blocks[k]:
            copy.wait()
        stacked = []
        for leaf in range(k * GROUP, k * GROUP + GROUP):
            high, low = parts_of(right[leaf])
            highs[leaf] = high
            lows[leaf] = low
            stacked += [high, high, low]
        here = matmul(jnp.concatenate(lefts[k * GROUP : k * GROUP + GROUP], 1), jnp.concatenate(stacked, 0))
        total = here if total is None else total + here
    cross, other_a, own_a, other_b, own_b = [total[:, j * LANES : (j + 1) * LANES] for j in range(5)]
    sent_a[...] = jnp.concatenate([cross, other_a], 1)
    kept_a[...] = jnp.concatenate([cross, own_a], 1)
    sent_b[...] = other_b
    kept_b[...] = own_b


def reduced(tiles, pattern, rhs, inverse, coupling, update):
    leaves, rows, columns = rhs.shape
    wide = columns + rows
    return pl.pallas_call(
        functools.partial(reduce_kernel, tiles),
        out_shape=(
            VMEM((rows, 2 * LANES), F32),
            VMEM((rows, 2 * LANES), F32),
            VMEM((rows, LANES), F32),
            VMEM((rows, LANES), F32),
            VMEM((leaves, rows, wide), BF16),
            VMEM((leaves, rows, wide), BF16),
            VMEM((leaves, rows, 3 * rows), BF16),
        ),
        in_specs=[pl.BlockSpec(memory_space=pltpu.SMEM)] + [IN_HBM] * 4,
        out_specs=(IN_VMEM,) * 7,
        scratch_shapes=[
            pltpu.VMEM((leaves, rows, wide), F32),
            pltpu.VMEM((leaves, rows, rows), F32),
            pltpu.VMEM((leaves, rows, rows), F32),
            pltpu.SemaphoreType.DMA((leaves // GROUP, 7)),
        ],
        compiler_params=pltpu.CompilerParams(vmem_limit_bytes=50 << 20),
    )(pattern, rhs, inverse, coupling, update)


def free_kernel(highs, lows, inverses, solved_a, solved_b, gains):
    for leaf in range(highs.shape[0]):
        high = highs[leaf]
        here = matmul(inverses[leaf], jnp.concatenate([high, high, lows[leaf]], 0))
        gains[leaf] = left_of(here[:, :LANES])
        solved_a[leaf] = here[:, LANES : 3 * LANES]
        solved_b[leaf] = here[:, 3 * LANES :]


def freed(highs, lows, inverses):
    leaves, rows, wide = highs.shape
    return pl.pallas_call(
        free_kernel,
        out_shape=(VMEM((leaves, rows, 2 * LANES), F32), VMEM((leaves, rows, 2 * LANES), F32), VMEM((leaves, rows, 3 * rows), BF16)),
        in_specs=[IN_VMEM] * 3,
        out_specs=(IN_VMEM,) * 3,
        compiler_params=pltpu.CompilerParams(vmem_limit_bytes=8 << 20),
        cost_estimate=pl.CostEstimate(flops=6 * leaves * rows * rows * wide, bytes_accessed=leaves * rows * wide * 8, transcendentals=0),
    )(highs, lows, inverses)


def small(kernel, out_shape, *operands):
    return pl.pallas_call(
        kernel,
        out_shape=out_shape,
        in_specs=[IN_VMEM] * len(operands),
        out_specs=jax.tree.map(lambda _: IN_VMEM, out_shape),
        compiler_params=pltpu.CompilerParams(vmem_limit_bytes=SMALL),
    )(*operands)


def map_kernel(tiles, received, kept, sep_rhs, sep_inverse, sep_coupling, mapped):
    start = starts(tiles, lax.rem(lax.axis_index("tile"), 2))[0]
    right = jnp.concatenate([sep_coupling[...], sep_rhs[:, lanes(start)]], 1)
    mapped[...] = product(sep_inverse[...], right - (received[...] + kept[...]))


def offset_kernel(tiles, received, kept, sep_rhs, sep_inverse, after, offset):
    start = starts(tiles, lax.rem(lax.axis_index("tile"), 2))[1]
    offset[...] = product(sep_inverse[...], sep_rhs[:, lanes(start)] - (received[...] + kept[...]))


def pair_kernel(mine_step, mine, other_step, other, after, whole):
    @pl.when(lax.rem(lax.axis_index("chain"), 2) == 1)
    def _():
        whole[...] = mine[...] - product(mine_step[...], other[...])

    @pl.when(lax.rem(lax.axis_index("chain"), 2) == 0)
    def _():
        whole[...] = other[...] - product(other_step[...], mine[...])


def carry_kernel(other_step, other, received, after, carry):
    section = lax.axis_index("chain")

    @pl.when(section == 0)
    def _():
        carry[...] = jnp.zeros_like(carry)

    @pl.when(section == 1)
    def _():
        carry[...] = other[...]

    @pl.when(section == 2)
    def _():
        carry[...] = received[...]

    @pl.when(section == 3)
    def _():
        carry[...] = other[...] - product(other_step[...], received[...])


def affine_kernel(step, block, offset, result):
    result[...] = offset[...] - product(step[...], block[...])


def affine(step, block, offset):
    return small(affine_kernel, VMEM(offset.shape, F32), step, block, offset)


def scanned(section, solved, half):
    sections = lax.axis_size("chain")
    whole_b, whole_a = solved[:, :half], solved[:, half:]
    before_b, before_a = jnp.zeros_like(whole_b), -jnp.eye(whole_a.shape[0], dtype=F32)
    nothing = jnp.zeros_like(whole_a)
    bit = 1
    while bit < sections:
        upper = (section // bit) % 2 == 1
        other = swapped(jnp.concatenate([whole_b, whole_a], 1), "chain", bit)
        other_b, other_a = other[:, :half], other[:, half:]
        before_b = jnp.where(upper, affine(before_a, other_b, before_b), before_b)
        before_a = jnp.where(upper, affine(before_a, other_a, nothing), before_a)
        first_b, first_a = jnp.where(upper, other_b, whole_b), jnp.where(upper, other_a, whole_a)
        second_b, second_a = jnp.where(upper, whole_b, other_b), jnp.where(upper, whole_a, other_a)
        whole_b = affine(second_a, first_b, second_b)
        whole_a = affine(second_a, first_a, nothing)
        bit *= 2
    return before_b


def last_kernel(tiles, chunk, solved, gains, theirs, mine, *refs):
    leaves = solved.shape[0]
    core = lax.rem(lax.axis_index("tile"), 2)
    order = [starts(tiles, 1 - core)[chunk], starts(tiles, core)[chunk]]
    copies = []
    if len(refs) > 4:
        step, offset_a, carry_a, offset_b, _, out, share_out, values, share, sems, share_sem = refs
        first = lax.axis_index("tile") < 2
        here = product(step[...], jnp.where(first, carry_a[...], mine[...]))
        share[...] = jnp.where(first, offset_a[...], offset_b[...]) - here
        copies.append(pltpu.make_async_copy(share, share_out, share_sem))
        copies[0].start()
    else:
        out, values, sems = refs[-3:]
    right = jnp.concatenate([right_of(theirs[...]), right_of(mine[...])], 1)
    for k in range(leaves // GROUP):
        for leaf in range(k * GROUP, k * GROUP + GROUP):
            values[leaf] = solved[leaf] - matmul(gains[leaf], right)
        some = pl.ds(k * GROUP, GROUP)
        for j, start in enumerate(order):
            copy = pltpu.make_async_copy(values.at[some, :, pl.ds(j * LANES, LANES)], out.at[some, :, lanes(start)], sems.at[k, j])
            copy.start()
            copies.append(copy)
    for copy in copies:
        copy.wait()


def leaf_values(tiles, chunk, solved, gains, theirs, mine, shared, *before):
    leaves, rows, width = solved.shape
    out_shape = [jax.ShapeDtypeStruct((leaves, rows, 2 * width), F32)]
    scratch = [pltpu.VMEM(solved.shape, F32)]
    sems = [pltpu.SemaphoreType.DMA((leaves // GROUP, 2))]
    if shared:
        out_shape.append(jax.ShapeDtypeStruct((rows, LANES), F32))
        scratch.append(pltpu.VMEM((rows, LANES), F32))
        sems.append(pltpu.SemaphoreType.DMA)
    return pl.pallas_call(
        functools.partial(last_kernel, tiles, chunk),
        out_shape=out_shape,
        in_specs=[IN_VMEM] * (4 + len(shared)) + [IN_HBM] * len(before),
        out_specs=[IN_HBM] * len(out_shape),
        scratch_shapes=scratch + sems,
        input_output_aliases={4 + len(shared): 0} if before else {},
        compiler_params=pltpu.CompilerParams(vmem_limit_bytes=8 << 20),
        cost_estimate=pl.CostEstimate(flops=6 * leaves * rows * rows * width, bytes_accessed=leaves * rows * width * 8, transcendentals=0),
    )(solved, gains, theirs, mine, *shared, *before)


def shards(
    leaf_rhs,
    leaf_inverse,
    leaf_coupling,
    leaf_update,
    update_pattern,
    sep_rhs,
    sep_inverse,
    sep_coupling,
):
    tiles = lax.axis_size("tile")
    sections = lax.axis_size("chain")
    tile = lax.axis_index("tile")
    section = lax.axis_index("chain")
    columns = sep_rhs.shape[2]
    width = columns // tiles
    block = VMEM((sep_rhs.shape[1], LANES), F32)
    double = VMEM((sep_rhs.shape[1], 2 * LANES), F32)

    sent_a, kept_a, sent_b, kept_b, highs, lows, inverses = reduced(
        tiles, update_pattern, leaf_rhs[0], leaf_inverse[0], leaf_coupling[0], leaf_update[0]
    )
    kept_a = kept_a + swapped(sent_a, "tile", 1)
    kept_b = kept_b + swapped(sent_b, "tile", 1)
    received_a = swapped(kept_a, "tile", 2) if tiles > 2 else jnp.zeros_like(kept_a)
    received_b = swapped(kept_b, "tile", 2) if tiles > 2 else jnp.zeros_like(kept_b)
    bit = 4
    while bit < tiles:
        kept_a, kept_b = kept_a + received_a, kept_b + received_b
        received_a, received_b = swapped(kept_a, "tile", bit), swapped(kept_b, "tile", bit)
        bit *= 2
    solved_a, solved_b, gains = freed(highs, lows, inverses)
    received_a, solved_a, solved_b, gains = lax.optimization_barrier((received_a, solved_a, solved_b, gains))
    mapped = small(functools.partial(map_kernel, tiles), double, received_a, kept_a, sep_rhs[0], sep_inverse[0], sep_coupling[0])
    offset_b = small(functools.partial(offset_kernel, tiles), block, received_b, kept_b, sep_rhs[0], sep_inverse[0], mapped)
    step, offset_a = mapped[:, :LANES], mapped[:, LANES:]
    if sections == 4:
        other = swapped(mapped, "chain", 1)
        other_step, other_a = other[:, :LANES], other[:, LANES:]
        other_b = swapped(offset_b, "chain", 1)
        whole_a = small(pair_kernel, block, step, offset_a, other_step, other_a, offset_b)
        met_a = swapped(whole_a, "chain", 2)
        whole_b = small(pair_kernel, block, step, offset_b, other_step, other_b, whole_a)
        met_b = swapped(whole_b, "chain", 2)
        carry_a = small(carry_kernel, block, other_step, other_a, met_a, whole_b)
        carry_b = small(carry_kernel, block, other_step, other_b, met_b, carry_a)
    else:
        carry = scanned(section, jnp.concatenate([offset_a, offset_b, step], 1), 2 * LANES)
        carry_a, carry_b = carry[:, :LANES], carry[:, LANES:]
    theirs_a = swapped(carry_a, "tile", 1)
    (leaf_share,) = leaf_values(tiles, 0, solved_a, gains, theirs_a, carry_a, ())
    theirs_b = swapped(carry_b, "tile", 1)
    if tiles == 4:
        shared = (step, offset_a, carry_a, offset_b)
        leaf_share, sep_share = leaf_values(tiles, 1, solved_b, gains, theirs_b, carry_b, shared, leaf_share)
    else:
        (leaf_share,) = leaf_values(tiles, 1, solved_b, gains, theirs_b, carry_b, (), leaf_share)
        own = affine(step, jnp.concatenate([carry_a, carry_b], 1), jnp.concatenate([offset_a, offset_b], 1))
        others = swapped(own, "tile", 1)
        lower = jnp.where(tile % 2 == 0, own, others)
        upper = jnp.where(tile % 2 == 0, others, own)
        sep_share = lax.dynamic_slice_in_dim(jnp.concatenate([lower, upper], 1), tile * width, width, 1)
    return (leaf_share[None], sep_share[None])


def solution(mesh):
    return jax.shard_map(
        shards,
        mesh=mesh,
        in_specs=(
            P(("parts", "chain"), "tile", None, None),
            P(("parts", "chain"), "tile", None, None),
            P(("parts", "chain"), "tile", None, None),
            P(("parts", "chain"), "tile", None, None),
            P(("parts", "chain"), "tile"),
            P(("parts", "chain"), None, None),
            P(("parts", "chain"), None, None),
            P(("parts", "chain"), None, None),
        ),
        out_specs=(P(("parts", "chain"), "tile", None, None), P(("parts", "chain"), None, "tile")),
        check_vma=False,
    )
```

```python
import functools

import jax
import jax.numpy as jnp
from jax import lax
from jax.experimental import pallas as pl
from jax.experimental.pallas import tpu as pltpu
from jax.sharding import PartitionSpec as P

F32 = jnp.float32
BF16 = jnp.bfloat16
LANES = 128
VMEM = pltpu.MemorySpace.VMEM
IN_VMEM = pl.BlockSpec(memory_space=pltpu.VMEM)
IN_HBM = pl.BlockSpec(memory_space=pl.ANY)
GROUP = 4
SMALL = 4 << 20


def swapped(block, axis, bit):
    route = [(i, i ^ bit) for i in range(lax.axis_size(axis))]
    return lax.ppermute(block, axis, route)


def parts_of(block):
    high = block.astype(BF16)
    return high, (block - high.astype(F32)).astype(BF16)


def matmul(left, right):
    return lax.dot_general(left, right, (((1,), (0,)), ((), ())), preferred_element_type=F32)


def left_of(block):
    high, low = parts_of(block)
    return jnp.concatenate([high, low, high], 1)


def right_of(block):
    high, low = parts_of(block)
    return jnp.concatenate([high, high, low], 0)


def product(left, right):
    return matmul(left_of(left), right_of(right))


def starts(tiles, which):
    if tiles == 4:
        return [which * LANES, which * LANES + 2 * LANES]
    return [which * 2 * LANES, which * 2 * LANES + LANES]


def lanes(start):
    return pl.ds(pl.multiple_of(start, LANES), LANES)


def fetched(rhs, starts_of, right, first, sems):
    rows = []
    for k in range(rhs.shape[0] // GROUP):
        some = pl.ds(k * GROUP, GROUP)
        row = []
        for j, start in enumerate(starts_of):
            row.append(pltpu.make_async_copy(rhs.at[some, :, lanes(start)], right.at[some, :, pl.ds((first + j) * LANES, LANES)], sems.at[k, first + j]))
        rows.append(row)
    return rows


def summed(lefts, right, highs, lows, copies):
    total = None
    for k, row in enumerate(copies):
        for copy in row:
            copy.wait()
        stacked = []
        for leaf in range(k * GROUP, k * GROUP + GROUP):
            high, low = parts_of(right[leaf])
            highs[leaf] = high
            lows[leaf] = low
            stacked += [high, high, low]
        here = matmul(lefts(k), jnp.concatenate(stacked, 0))
        total = here if total is None else total + here
    return total


def reduce_kernel(tiles, pattern, rhs, inverse, coupling, update, sent, kept, lefts, highs, lows, inverses, rest, right, tiles_a, tiles_b, flags, sems, sems_r, sems_b, flag_sem):
    leaves, rows = rhs.shape[:2]
    core = lax.rem(lax.axis_index("tile"), 2)
    flag_copy = pltpu.make_async_copy(pattern, flags, flag_sem)
    flag_copy.start()
    other, own = starts(tiles, 1 - core), starts(tiles, core)
    copies = []
    for k in range(leaves // GROUP):
        some = pl.ds(k * GROUP, GROUP)
        pair = [
            pltpu.make_async_copy(update.at[some], tiles_a.at[some], sems.at[k, 0]),
            pltpu.make_async_copy(inverse.at[some], tiles_b.at[some], sems.at[k, 1]),
        ]
        for copy in pair:
            copy.start()
        copies.append(pair)
    blocks = fetched(rhs, [other[0], own[0]], right, 1, sems_r)
    for k, row in enumerate(blocks):
        some = pl.ds(k * GROUP, GROUP)
        row.insert(0, pltpu.make_async_copy(coupling.at[some], right.at[some, :, pl.ds(0, LANES)], sems_r.at[k, 0]))
    later = fetched(rhs, [other[1], own[1]], rest, 0, sems_b)
    flag_copy.wait()
    for k in range(leaves // GROUP):
        for copy in copies[k]:
            copy.wait()
        for copy in blocks[k]:
            copy.start()
        for leaf in range(k * GROUP, k * GROUP + GROUP):
            inv_high, inv_low = parts_of(tiles_b[leaf])
            inverses[leaf] = jnp.concatenate([inv_high, inv_low, inv_high], 1)
            masked = tiles_a[leaf] * flags[0, leaf].astype(F32)
            here = matmul(left_of(masked), jnp.concatenate([inv_high, inv_high, inv_low], 0))
            lefts[:, pl.ds(leaf * 3 * rows, 3 * rows)] = left_of(here)
    total = None
    for k, row in enumerate(blocks):
        for copy in row:
            copy.wait()
        for copy in later[k]:
            copy.start()
        here = summed(lefts, right, highs, lows, k)
        total = here if total is None else total + here
    sent[...] = total[:, : 2 * LANES]
    kept[...] = jnp.concatenate([total[:, :LANES], total[:, 2 * LANES :]], 1)
    for row in later:
        for copy in row:
            copy.wait()


def summed(lefts, right, highs, lows, k):
    rows = lefts.shape[0]
    span = GROUP * 3 * rows
    stacked = []
    for leaf in range(k * GROUP, k * GROUP + GROUP):
        high, low = parts_of(right[leaf])
        highs[leaf] = high
        lows[leaf] = low
        stacked += [high, high, low]
    return matmul(lefts[:, pl.ds(k * span, span)], jnp.concatenate(stacked, 0))


def reduced(tiles, pattern, rhs, inverse, coupling, update):
    leaves, rows, columns = rhs.shape
    half = columns // 2
    wide = rows + half
    return pl.pallas_call(
        functools.partial(reduce_kernel, tiles),
        out_shape=(
            VMEM((rows, 2 * LANES), F32),
            VMEM((rows, 2 * LANES), F32),
            VMEM((rows, leaves * 3 * rows), BF16),
            VMEM((leaves, rows, wide), BF16),
            VMEM((leaves, rows, wide), BF16),
            VMEM((leaves, rows, 3 * rows), BF16),
            VMEM((leaves, rows, half), F32),
        ),
        in_specs=[IN_HBM] * 5,
        out_specs=(IN_VMEM,) * 7,
        scratch_shapes=[
            pltpu.VMEM((leaves, rows, wide), F32),
            pltpu.VMEM((leaves, rows, rows), F32),
            pltpu.VMEM((leaves, rows, rows), F32),
            pltpu.SMEM(pattern.shape, jnp.int32),
            pltpu.SemaphoreType.DMA((leaves // GROUP, 2)),
            pltpu.SemaphoreType.DMA((leaves // GROUP, 3)),
            pltpu.SemaphoreType.DMA((leaves // GROUP, 2)),
            pltpu.SemaphoreType.DMA,
        ],
        compiler_params=pltpu.CompilerParams(vmem_limit_bytes=48 << 20),
    )(pattern, rhs, inverse, coupling, update)


def second_kernel(lefts, rest, sent, kept, highs, lows):
    total = None
    for k in range(rest.shape[0] // GROUP):
        here = summed(lefts, rest, highs, lows, k)
        total = here if total is None else total + here
    sent[...] = total[:, :LANES]
    kept[...] = total[:, LANES:]


def second_reduced(lefts, rest):
    leaves, rows, half = rest.shape
    return pl.pallas_call(
        second_kernel,
        out_shape=(
            VMEM((rows, LANES), F32),
            VMEM((rows, LANES), F32),
            VMEM((leaves, rows, half), BF16),
            VMEM((leaves, rows, half), BF16),
        ),
        in_specs=[IN_VMEM] * 2,
        out_specs=(IN_VMEM,) * 4,
        compiler_params=pltpu.CompilerParams(vmem_limit_bytes=8 << 20),
        cost_estimate=pl.CostEstimate(flops=6 * leaves * rows * rows * half, bytes_accessed=leaves * rows * half * 8, transcendentals=0),
    )(lefts, rest)


def free_kernel(highs_a, lows_a, highs_b, lows_b, inverses, after, solved_a, solved_b, gains, token):
    for leaf in range(highs_a.shape[0]):
        left = inverses[leaf]
        high = highs_a[leaf]
        here = matmul(left, jnp.concatenate([high, high, lows_a[leaf]], 0))
        gains[leaf] = left_of(here[:, :LANES])
        solved_a[leaf] = here[:, LANES:]
        high = highs_b[leaf]
        solved_b[leaf] = matmul(left, jnp.concatenate([high, high, lows_b[leaf]], 0))
    token[...] = jnp.zeros_like(token)


def freed(highs_a, lows_a, highs_b, lows_b, inverses, after):
    leaves, rows, wide = highs_a.shape
    half = highs_b.shape[2]
    return pl.pallas_call(
        free_kernel,
        out_shape=(
            VMEM((leaves, rows, half), F32),
            VMEM((leaves, rows, half), F32),
            VMEM((leaves, rows, 3 * rows), BF16),
            VMEM((8, LANES), F32),
        ),
        in_specs=[IN_VMEM] * 6,
        out_specs=(IN_VMEM,) * 4,
        compiler_params=pltpu.CompilerParams(vmem_limit_bytes=8 << 20),
        cost_estimate=pl.CostEstimate(flops=6 * leaves * rows * rows * (wide + half), bytes_accessed=leaves * rows * wide * 12, transcendentals=0),
    )(highs_a, lows_a, highs_b, lows_b, inverses, after)


def small(kernel, out_shape, *operands):
    return pl.pallas_call(
        kernel,
        out_shape=out_shape,
        in_specs=[IN_VMEM] * len(operands),
        out_specs=jax.tree.map(lambda _: IN_VMEM, out_shape),
        compiler_params=pltpu.CompilerParams(vmem_limit_bytes=SMALL),
    )(*operands)


def map_kernel(tiles, received, kept, sep_rhs, sep_inverse, sep_coupling, mapped):
    start = starts(tiles, lax.rem(lax.axis_index("tile"), 2))[0]
    right = jnp.concatenate([sep_coupling[...], sep_rhs[:, lanes(start)]], 1)
    mapped[...] = product(sep_inverse[...], right - (received[...] + kept[...]))


def offset_kernel(tiles, received, kept, sep_rhs, sep_inverse, after, offset):
    start = starts(tiles, lax.rem(lax.axis_index("tile"), 2))[1]
    offset[...] = product(sep_inverse[...], sep_rhs[:, lanes(start)] - (received[...] + kept[...]))


def pair_kernel(mine_step, mine, other_step, other, after, whole):
    @pl.when(lax.rem(lax.axis_index("chain"), 2) == 1)
    def _():
        whole[...] = mine[...] - product(mine_step[...], other[...])

    @pl.when(lax.rem(lax.axis_index("chain"), 2) == 0)
    def _():
        whole[...] = other[...] - product(other_step[...], mine[...])


def carry_kernel(other_step, other, received, after, carry):
    section = lax.axis_index("chain")

    @pl.when(section == 0)
    def _():
        carry[...] = jnp.zeros_like(carry)

    @pl.when(section == 1)
    def _():
        carry[...] = other[...]

    @pl.when(section == 2)
    def _():
        carry[...] = received[...]

    @pl.when(section == 3)
    def _():
        carry[...] = other[...] - product(other_step[...], received[...])


def affine_kernel(step, block, offset, result):
    result[...] = offset[...] - product(step[...], block[...])


def affine(step, block, offset):
    return small(affine_kernel, VMEM(offset.shape, F32), step, block, offset)


def scanned(section, solved, half):
    sections = lax.axis_size("chain")
    whole_b, whole_a = solved[:, :half], solved[:, half:]
    before_b, before_a = jnp.zeros_like(whole_b), -jnp.eye(whole_a.shape[0], dtype=F32)
    nothing = jnp.zeros_like(whole_a)
    bit = 1
    while bit < sections:
        upper = (section // bit) % 2 == 1
        other = swapped(jnp.concatenate([whole_b, whole_a], 1), "chain", bit)
        other_b, other_a = other[:, :half], other[:, half:]
        before_b = jnp.where(upper, affine(before_a, other_b, before_b), before_b)
        before_a = jnp.where(upper, affine(before_a, other_a, nothing), before_a)
        first_b, first_a = jnp.where(upper, other_b, whole_b), jnp.where(upper, other_a, whole_a)
        second_b, second_a = jnp.where(upper, whole_b, other_b), jnp.where(upper, whole_a, other_a)
        whole_b = affine(second_a, first_b, second_b)
        whole_a = affine(second_a, first_a, nothing)
        bit *= 2
    return before_b


def last_kernel(tiles, blocks, shared, first, gains, *refs):
    leaves, rows = gains.shape[:2]
    count = len(blocks)
    core = lax.rem(lax.axis_index("tile"), 2)
    solved, carries, refs = refs[:count], refs[count : 2 * count], refs[2 * count :]
    copies = []
    if shared:
        step, offset_a, carry_a, offset_b, carry_b = refs[:5]
        out, share_out, values, sems, share, share_sem = refs[-6:]
        low = lax.axis_index("tile") < 2
        here = product(step[...], jnp.where(low, carry_a[...], carry_b[...]))
        share[...] = jnp.where(low, offset_a[...], offset_b[...]) - here
        copies.append(pltpu.make_async_copy(share, share_out, share_sem))
        copies[0].start()
    else:
        out, values, sems = refs[-4] if first else refs[-3], refs[-2], refs[-1]
    places = [starts(tiles, core if own else 1 - core)[chunk] for chunk, own in blocks]
    right = jnp.concatenate([right_of(carry[...]) for carry in carries], 1)
    for k in range(leaves // GROUP):
        for leaf in range(k * GROUP, k * GROUP + GROUP):
            here = matmul(gains[leaf], right)
            for j, (_, own) in enumerate(blocks):
                side = pl.ds(LANES if own else 0, LANES)
                values[j, leaf] = solved[j][leaf, :, side] - here[:, j * LANES : (j + 1) * LANES]
        some = pl.ds(k * GROUP, GROUP)
        for j, start in enumerate(places):
            copy = pltpu.make_async_copy(values.at[j, some], out.at[some, :, lanes(start)], sems.at[k, j])
            copy.start()
            copies.append(copy)
    if first:
        refs[-3][...] = jnp.zeros_like(refs[-3])
    for copy in copies:
        copy.wait()


def leaf_values(tiles, blocks, columns, gains, solved, carries, shared, *before):
    leaves, rows = gains.shape[:2]
    count = len(blocks)
    out_shape = [jax.ShapeDtypeStruct((leaves, rows, columns), F32)]
    out_specs = [IN_HBM]
    if not before:
        out_shape.append(VMEM((8, LANES), F32))
        out_specs.append(IN_VMEM)
    scratch = [pltpu.VMEM((count, leaves, rows, LANES), F32), pltpu.SemaphoreType.DMA((leaves // GROUP, count))]
    if shared:
        out_shape.append(jax.ShapeDtypeStruct((rows, LANES), F32))
        out_specs.append(IN_HBM)
        scratch += [pltpu.VMEM((rows, LANES), F32), pltpu.SemaphoreType.DMA]
    operands = 1 + 2 * count + len(shared)
    return pl.pallas_call(
        functools.partial(last_kernel, tiles, blocks, bool(shared), not before),
        out_shape=out_shape,
        in_specs=[IN_VMEM] * operands + [IN_HBM] * len(before),
        out_specs=out_specs,
        scratch_shapes=scratch,
        input_output_aliases={operands: 0} if before else {},
        compiler_params=pltpu.CompilerParams(vmem_limit_bytes=8 << 20),
        cost_estimate=pl.CostEstimate(flops=6 * leaves * rows * rows * LANES * count, bytes_accessed=leaves * rows * LANES * count * 8, transcendentals=0),
    )(gains, *solved, *carries, *shared, *before)


def shards(
    leaf_rhs,
    leaf_inverse,
    leaf_coupling,
    leaf_update,
    update_pattern,
    sep_rhs,
    sep_inverse,
    sep_coupling,
):
    tiles = lax.axis_size("tile")
    sections = lax.axis_size("chain")
    tile = lax.axis_index("tile")
    section = lax.axis_index("chain")
    columns = sep_rhs.shape[2]
    width = columns // tiles
    block = VMEM((sep_rhs.shape[1], LANES), F32)
    double = VMEM((sep_rhs.shape[1], 2 * LANES), F32)
    inverse, right = sep_inverse[0], sep_rhs[0]

    sent_a, kept_a, lefts, highs_a, lows_a, inverses, rest = reduced(
        tiles, update_pattern, leaf_rhs[0], leaf_inverse[0], leaf_coupling[0], leaf_update[0]
    )
    kept_a = kept_a + swapped(sent_a, "tile", 1)
    sent_b, kept_b, highs_b, lows_b = second_reduced(lefts, rest)
    kept_b = kept_b + swapped(sent_b, "tile", 1)
    received_a = swapped(kept_a, "tile", 2) if tiles > 2 else jnp.zeros_like(kept_a)
    received_b = swapped(kept_b, "tile", 2) if tiles > 2 else jnp.zeros_like(kept_b)
    bit = 4
    while bit < tiles:
        kept_a, kept_b = kept_a + received_a, kept_b + received_b
        received_a, received_b = swapped(kept_a, "tile", bit), swapped(kept_b, "tile", bit)
        bit *= 2
    mapped = small(functools.partial(map_kernel, tiles), double, received_a, kept_a, right, inverse, sep_coupling[0])
    offset_b = small(functools.partial(offset_kernel, tiles), block, received_b, kept_b, right, inverse, mapped)
    step, offset_a = mapped[:, :LANES], mapped[:, LANES:]
    if sections == 4:
        other = swapped(mapped, "chain", 1)
        other_step, other_a = other[:, :LANES], other[:, LANES:]
        other_b = swapped(offset_b, "chain", 1)
        whole_a = small(pair_kernel, block, step, offset_a, other_step, other_a, offset_b)
        met_a = swapped(whole_a, "chain", 2)
        whole_b = small(pair_kernel, block, step, offset_b, other_step, other_b, whole_a)
        met_b = swapped(whole_b, "chain", 2)
        solved_a, solved_b, gains, token = freed(highs_a, lows_a, highs_b, lows_b, inverses, whole_b)
        carry_a = small(carry_kernel, block, other_step, other_a, met_a, token)
        leaf_share, token = leaf_values(tiles, ((0, True),), columns, gains, [solved_a], [carry_a], ())
        carry_b = small(carry_kernel, block, other_step, other_b, met_b, token)
    else:
        solved_a, solved_b, gains, _ = freed(highs_a, lows_a, highs_b, lows_b, inverses, mapped)
        carry = scanned(section, jnp.concatenate([offset_a, offset_b, step], 1), 2 * LANES)
        carry_a, carry_b = carry[:, :LANES], carry[:, LANES:]
        leaf_share, _ = leaf_values(tiles, ((0, True),), columns, gains, [solved_a], [carry_a], ())
    theirs_a = swapped(carry_a, "tile", 1)
    theirs_b = swapped(carry_b, "tile", 1)
    shared = (step, offset_a, carry_a, offset_b, carry_b) if tiles == 4 else ()
    middle = leaf_values(tiles, ((0, False), (1, True)), columns, gains, [solved_a, solved_b], [theirs_a, carry_b], shared, leaf_share)
    (leaf_share,) = leaf_values(tiles, ((1, False),), columns, gains, [solved_b], [theirs_b], (), middle[0])
    if tiles == 4:
        sep_share = middle[1]
    else:
        own = affine(step, jnp.concatenate([carry_a, carry_b], 1), jnp.concatenate([offset_a, offset_b], 1))
        others = swapped(own, "tile", 1)
        lower = jnp.where(tile % 2 == 0, own, others)
        upper = jnp.where(tile % 2 == 0, others, own)
        sep_share = lax.dynamic_slice_in_dim(jnp.concatenate([lower, upper], 1), tile * width, width, 1)
    return (leaf_share[None], sep_share[None])


def solution(mesh):
    return jax.shard_map(
        shards,
        mesh=mesh,
        in_specs=(
            P(("parts", "chain"), "tile", None, None),
            P(("parts", "chain"), "tile", None, None),
            P(("parts", "chain"), "tile", None, None),
            P(("parts", "chain"), "tile", None, None),
            P(("parts", "chain"), "tile"),
            P(("parts", "chain"), None, None),
            P(("parts", "chain"), None, None),
            P(("parts", "chain"), None, None),
        ),
        out_specs=(P(("parts", "chain"), "tile", None, None), P(("parts", "chain"), None, "tile")),
        check_vma=False,
    )
```

```python
import functools

import jax
import jax.numpy as jnp
from jax import lax
from jax.experimental import pallas as pl
from jax.experimental.pallas import tpu as pltpu
from jax.sharding import PartitionSpec as P

F32 = jnp.float32
BF16 = jnp.bfloat16
LANES = 128
VMEM = pltpu.MemorySpace.VMEM
IN_VMEM = pl.BlockSpec(memory_space=pltpu.VMEM)
IN_HBM = pl.BlockSpec(memory_space=pl.ANY)
GROUP = 4
SMALL = 4 << 20


def swapped(block, axis, bit):
    route = [(i, i ^ bit) for i in range(lax.axis_size(axis))]
    return lax.ppermute(block, axis, route)


def parts_of(block):
    high = block.astype(BF16)
    return high, (block - high.astype(F32)).astype(BF16)


def matmul(left, right):
    return lax.dot_general(left, right, (((1,), (0,)), ((), ())), preferred_element_type=F32)


def left_of(block):
    high, low = parts_of(block)
    return jnp.concatenate([high, low, high], 1)


def right_of(block):
    high, low = parts_of(block)
    return jnp.concatenate([high, high, low], 0)


def product(left, right):
    return matmul(left_of(left), right_of(right))


def starts(tiles, which):
    if tiles == 4:
        return [which * LANES, which * LANES + 2 * LANES]
    return [which * 2 * LANES, which * 2 * LANES + LANES]


def lanes(start):
    return pl.ds(pl.multiple_of(start, LANES), LANES)


def fetched(rhs, starts_of, right, first, sems):
    rows = []
    for k in range(rhs.shape[0] // GROUP):
        some = pl.ds(k * GROUP, GROUP)
        row = []
        for j, start in enumerate(starts_of):
            row.append(pltpu.make_async_copy(rhs.at[some, :, lanes(start)], right.at[some, :, pl.ds((first + j) * LANES, LANES)], sems.at[k, first + j]))
        rows.append(row)
    return rows


def summed(lefts, right, highs, lows, copies):
    total = None
    for k, row in enumerate(copies):
        for copy in row:
            copy.wait()
        stacked = []
        for leaf in range(k * GROUP, k * GROUP + GROUP):
            high, low = parts_of(right[leaf])
            highs[leaf] = high
            lows[leaf] = low
            stacked += [high, high, low]
        here = matmul(lefts(k), jnp.concatenate(stacked, 0))
        total = here if total is None else total + here
    return total


def reduce_kernel(tiles, pattern, rhs, inverse, coupling, update, sent, kept, lefts, highs, lows, inverses, rest, right, tiles_a, tiles_b, flags, sems, sems_r, sems_b, flag_sem):
    leaves, rows = rhs.shape[:2]
    core = lax.rem(lax.axis_index("tile"), 2)
    flag_copy = pltpu.make_async_copy(pattern, flags, flag_sem)
    flag_copy.start()
    other, own = starts(tiles, 1 - core), starts(tiles, core)
    copies = []
    for k in range(leaves // GROUP):
        some = pl.ds(k * GROUP, GROUP)
        pair = [
            pltpu.make_async_copy(update.at[some], tiles_a.at[some], sems.at[k, 0]),
            pltpu.make_async_copy(inverse.at[some], tiles_b.at[some], sems.at[k, 1]),
        ]
        for copy in pair:
            copy.start()
        copies.append(pair)
    blocks = fetched(rhs, [other[0], own[0]], right, 1, sems_r)
    for k, row in enumerate(blocks):
        some = pl.ds(k * GROUP, GROUP)
        row.insert(0, pltpu.make_async_copy(coupling.at[some], right.at[some, :, pl.ds(0, LANES)], sems_r.at[k, 0]))
    for row in blocks[:2]:
        for copy in row:
            copy.start()
    later = fetched(rhs, [other[1], own[1]], rest, 0, sems_b)
    flag_copy.wait()
    for k in range(leaves // GROUP):
        for copy in copies[k]:
            copy.wait()
        for copy in blocks[k + 2] if k + 2 < len(blocks) else later[k + 2 - len(blocks)]:
            copy.start()
        for leaf in range(k * GROUP, k * GROUP + GROUP):
            inv_high, inv_low = parts_of(tiles_b[leaf])
            inverses[leaf] = jnp.concatenate([inv_high, inv_low, inv_high], 1)
            masked = tiles_a[leaf] * flags[0, leaf].astype(F32)
            here = matmul(left_of(masked), jnp.concatenate([inv_high, inv_high, inv_low], 0))
            lefts[:, pl.ds(leaf * 3 * rows, 3 * rows)] = left_of(here)
    total = None
    for k, row in enumerate(blocks):
        for copy in row:
            copy.wait()
        if k + 2 < len(later):
            for copy in later[k + 2]:
                copy.start()
        here = summed(lefts, right, highs, lows, k)
        total = here if total is None else total + here
    sent[...] = total[:, : 2 * LANES]
    kept[...] = jnp.concatenate([total[:, :LANES], total[:, 2 * LANES :]], 1)
    for row in later:
        for copy in row:
            copy.wait()


def summed(lefts, right, highs, lows, k):
    rows = lefts.shape[0]
    span = GROUP * 3 * rows
    stacked = []
    for leaf in range(k * GROUP, k * GROUP + GROUP):
        high, low = parts_of(right[leaf])
        highs[leaf] = high
        lows[leaf] = low
        stacked += [high, high, low]
    return matmul(lefts[:, pl.ds(k * span, span)], jnp.concatenate(stacked, 0))


def reduced(tiles, pattern, rhs, inverse, coupling, update):
    leaves, rows, columns = rhs.shape
    half = columns // 2
    wide = rows + half
    return pl.pallas_call(
        functools.partial(reduce_kernel, tiles),
        out_shape=(
            VMEM((rows, 2 * LANES), F32),
            VMEM((rows, 2 * LANES), F32),
            VMEM((rows, leaves * 3 * rows), BF16),
            VMEM((leaves, rows, wide), BF16),
            VMEM((leaves, rows, wide), BF16),
            VMEM((leaves, rows, 3 * rows), BF16),
            VMEM((leaves, rows, half), F32),
        ),
        in_specs=[IN_HBM] * 5,
        out_specs=(IN_VMEM,) * 7,
        scratch_shapes=[
            pltpu.VMEM((leaves, rows, wide), F32),
            pltpu.VMEM((leaves, rows, rows), F32),
            pltpu.VMEM((leaves, rows, rows), F32),
            pltpu.SMEM(pattern.shape, jnp.int32),
            pltpu.SemaphoreType.DMA((leaves // GROUP, 2)),
            pltpu.SemaphoreType.DMA((leaves // GROUP, 3)),
            pltpu.SemaphoreType.DMA((leaves // GROUP, 2)),
            pltpu.SemaphoreType.DMA,
        ],
        compiler_params=pltpu.CompilerParams(vmem_limit_bytes=48 << 20),
    )(pattern, rhs, inverse, coupling, update)


def second_kernel(lefts, rest, sent, kept, highs, lows):
    total = None
    for k in range(rest.shape[0] // GROUP):
        here = summed(lefts, rest, highs, lows, k)
        total = here if total is None else total + here
    sent[...] = total[:, :LANES]
    kept[...] = total[:, LANES:]


def second_reduced(lefts, rest):
    leaves, rows, half = rest.shape
    return pl.pallas_call(
        second_kernel,
        out_shape=(
            VMEM((rows, LANES), F32),
            VMEM((rows, LANES), F32),
            VMEM((leaves, rows, half), BF16),
            VMEM((leaves, rows, half), BF16),
        ),
        in_specs=[IN_VMEM] * 2,
        out_specs=(IN_VMEM,) * 4,
        compiler_params=pltpu.CompilerParams(vmem_limit_bytes=8 << 20),
        cost_estimate=pl.CostEstimate(flops=6 * leaves * rows * rows * half, bytes_accessed=leaves * rows * half * 8, transcendentals=0),
    )(lefts, rest)


def free_kernel(highs_a, lows_a, highs_b, lows_b, inverses, after, solved_a, solved_b, gains, token):
    for leaf in range(highs_a.shape[0]):
        left = inverses[leaf]
        high = highs_a[leaf]
        here = matmul(left, jnp.concatenate([high, high, lows_a[leaf]], 0))
        gains[leaf] = left_of(here[:, :LANES])
        solved_a[leaf] = here[:, LANES:]
        high = highs_b[leaf]
        solved_b[leaf] = matmul(left, jnp.concatenate([high, high, lows_b[leaf]], 0))
    token[...] = jnp.zeros_like(token)


def freed(highs_a, lows_a, highs_b, lows_b, inverses, after):
    leaves, rows, wide = highs_a.shape
    half = highs_b.shape[2]
    return pl.pallas_call(
        free_kernel,
        out_shape=(
            VMEM((leaves, rows, half), F32),
            VMEM((leaves, rows, half), F32),
            VMEM((leaves, rows, 3 * rows), BF16),
            VMEM((8, LANES), F32),
        ),
        in_specs=[IN_VMEM] * 6,
        out_specs=(IN_VMEM,) * 4,
        compiler_params=pltpu.CompilerParams(vmem_limit_bytes=8 << 20),
        cost_estimate=pl.CostEstimate(flops=6 * leaves * rows * rows * (wide + half), bytes_accessed=leaves * rows * wide * 12, transcendentals=0),
    )(highs_a, lows_a, highs_b, lows_b, inverses, after)


def small(kernel, out_shape, *operands):
    return pl.pallas_call(
        kernel,
        out_shape=out_shape,
        in_specs=[IN_VMEM] * len(operands),
        out_specs=jax.tree.map(lambda _: IN_VMEM, out_shape),
        compiler_params=pltpu.CompilerParams(vmem_limit_bytes=SMALL),
    )(*operands)


def map_kernel(tiles, received, kept, sep_rhs, sep_inverse, sep_coupling, mapped):
    start = starts(tiles, lax.rem(lax.axis_index("tile"), 2))[0]
    right = jnp.concatenate([sep_coupling[...], sep_rhs[:, lanes(start)]], 1)
    mapped[...] = product(sep_inverse[...], right - (received[...] + kept[...]))


def offset_kernel(tiles, received, kept, sep_rhs, sep_inverse, after, offset):
    start = starts(tiles, lax.rem(lax.axis_index("tile"), 2))[1]
    offset[...] = product(sep_inverse[...], sep_rhs[:, lanes(start)] - (received[...] + kept[...]))


def pair_kernel(mine_step, mine, other_step, other, after, whole):
    @pl.when(lax.rem(lax.axis_index("chain"), 2) == 1)
    def _():
        whole[...] = mine[...] - product(mine_step[...], other[...])

    @pl.when(lax.rem(lax.axis_index("chain"), 2) == 0)
    def _():
        whole[...] = other[...] - product(other_step[...], mine[...])


def carry_kernel(other_step, other, received, after, carry):
    section = lax.axis_index("chain")

    @pl.when(section == 0)
    def _():
        carry[...] = jnp.zeros_like(carry)

    @pl.when(section == 1)
    def _():
        carry[...] = other[...]

    @pl.when(section == 2)
    def _():
        carry[...] = received[...]

    @pl.when(section == 3)
    def _():
        carry[...] = other[...] - product(other_step[...], received[...])


def affine_kernel(step, block, offset, result):
    result[...] = offset[...] - product(step[...], block[...])


def affine(step, block, offset):
    return small(affine_kernel, VMEM(offset.shape, F32), step, block, offset)


def scanned(section, solved, half):
    sections = lax.axis_size("chain")
    whole_b, whole_a = solved[:, :half], solved[:, half:]
    before_b, before_a = jnp.zeros_like(whole_b), -jnp.eye(whole_a.shape[0], dtype=F32)
    nothing = jnp.zeros_like(whole_a)
    bit = 1
    while bit < sections:
        upper = (section // bit) % 2 == 1
        other = swapped(jnp.concatenate([whole_b, whole_a], 1), "chain", bit)
        other_b, other_a = other[:, :half], other[:, half:]
        before_b = jnp.where(upper, affine(before_a, other_b, before_b), before_b)
        before_a = jnp.where(upper, affine(before_a, other_a, nothing), before_a)
        first_b, first_a = jnp.where(upper, other_b, whole_b), jnp.where(upper, other_a, whole_a)
        second_b, second_a = jnp.where(upper, whole_b, other_b), jnp.where(upper, whole_a, other_a)
        whole_b = affine(second_a, first_b, second_b)
        whole_a = affine(second_a, first_a, nothing)
        bit *= 2
    return before_b


def last_kernel(tiles, blocks, shared, first, gains, *refs):
    leaves, rows = gains.shape[:2]
    count = len(blocks)
    core = lax.rem(lax.axis_index("tile"), 2)
    solved, carries, refs = refs[:count], refs[count : 2 * count], refs[2 * count :]
    copies = []
    if shared:
        step, offset_a, carry_a, offset_b, carry_b = refs[:5]
        out, share_out, values, sems, share, share_sem = refs[-6:]
        low = lax.axis_index("tile") < 2
        here = product(step[...], jnp.where(low, carry_a[...], carry_b[...]))
        share[...] = jnp.where(low, offset_a[...], offset_b[...]) - here
        copies.append(pltpu.make_async_copy(share, share_out, share_sem))
        copies[0].start()
    else:
        out, values, sems = refs[-4] if first else refs[-3], refs[-2], refs[-1]
    places = [starts(tiles, core if own else 1 - core)[chunk] for chunk, own in blocks]
    right = jnp.concatenate([right_of(carry[...]) for carry in carries], 1)
    for k in range(leaves // GROUP):
        for leaf in range(k * GROUP, k * GROUP + GROUP):
            here = matmul(gains[leaf], right)
            for j, (_, own) in enumerate(blocks):
                side = pl.ds(LANES if own else 0, LANES)
                values[j, leaf] = solved[j][leaf, :, side] - here[:, j * LANES : (j + 1) * LANES]
        some = pl.ds(k * GROUP, GROUP)
        for j, start in enumerate(places):
            copy = pltpu.make_async_copy(values.at[j, some], out.at[some, :, lanes(start)], sems.at[k, j])
            copy.start()
            copies.append(copy)
    if first:
        refs[-3][...] = jnp.zeros_like(refs[-3])
    for copy in copies:
        copy.wait()


def leaf_values(tiles, blocks, columns, gains, solved, carries, shared, *before):
    leaves, rows = gains.shape[:2]
    count = len(blocks)
    out_shape = [jax.ShapeDtypeStruct((leaves, rows, columns), F32)]
    out_specs = [IN_HBM]
    if not before:
        out_shape.append(VMEM((8, LANES), F32))
        out_specs.append(IN_VMEM)
    scratch = [pltpu.VMEM((count, leaves, rows, LANES), F32), pltpu.SemaphoreType.DMA((leaves // GROUP, count))]
    if shared:
        out_shape.append(jax.ShapeDtypeStruct((rows, LANES), F32))
        out_specs.append(IN_HBM)
        scratch += [pltpu.VMEM((rows, LANES), F32), pltpu.SemaphoreType.DMA]
    operands = 1 + 2 * count + len(shared)
    return pl.pallas_call(
        functools.partial(last_kernel, tiles, blocks, bool(shared), not before),
        out_shape=out_shape,
        in_specs=[IN_VMEM] * operands + [IN_HBM] * len(before),
        out_specs=out_specs,
        scratch_shapes=scratch,
        input_output_aliases={operands: 0} if before else {},
        compiler_params=pltpu.CompilerParams(vmem_limit_bytes=8 << 20),
        cost_estimate=pl.CostEstimate(flops=6 * leaves * rows * rows * LANES * count, bytes_accessed=leaves * rows * LANES * count * 8, transcendentals=0),
    )(gains, *solved, *carries, *shared, *before)


def shards(
    leaf_rhs,
    leaf_inverse,
    leaf_coupling,
    leaf_update,
    update_pattern,
    sep_rhs,
    sep_inverse,
    sep_coupling,
):
    tiles = lax.axis_size("tile")
    sections = lax.axis_size("chain")
    tile = lax.axis_index("tile")
    section = lax.axis_index("chain")
    columns = sep_rhs.shape[2]
    width = columns // tiles
    block = VMEM((sep_rhs.shape[1], LANES), F32)
    double = VMEM((sep_rhs.shape[1], 2 * LANES), F32)
    inverse, right = sep_inverse[0], sep_rhs[0]

    sent_a, kept_a, lefts, highs_a, lows_a, inverses, rest = reduced(
        tiles, update_pattern, leaf_rhs[0], leaf_inverse[0], leaf_coupling[0], leaf_update[0]
    )
    kept_a = kept_a + swapped(sent_a, "tile", 1)
    sent_b, kept_b, highs_b, lows_b = second_reduced(lefts, rest)
    kept_b = kept_b + swapped(sent_b, "tile", 1)
    received_a = swapped(kept_a, "tile", 2) if tiles > 2 else jnp.zeros_like(kept_a)
    received_b = swapped(kept_b, "tile", 2) if tiles > 2 else jnp.zeros_like(kept_b)
    bit = 4
    while bit < tiles:
        kept_a, kept_b = kept_a + received_a, kept_b + received_b
        received_a, received_b = swapped(kept_a, "tile", bit), swapped(kept_b, "tile", bit)
        bit *= 2
    mapped = small(functools.partial(map_kernel, tiles), double, received_a, kept_a, right, inverse, sep_coupling[0])
    offset_b = small(functools.partial(offset_kernel, tiles), block, received_b, kept_b, right, inverse, mapped)
    step, offset_a = mapped[:, :LANES], mapped[:, LANES:]
    if sections == 4:
        other = swapped(mapped, "chain", 1)
        other_step, other_a = other[:, :LANES], other[:, LANES:]
        other_b = swapped(offset_b, "chain", 1)
        whole_a = small(pair_kernel, block, step, offset_a, other_step, other_a, offset_b)
        met_a = swapped(whole_a, "chain", 2)
        whole_b = small(pair_kernel, block, step, offset_b, other_step, other_b, whole_a)
        met_b = swapped(whole_b, "chain", 2)
        solved_a, solved_b, gains, token = freed(highs_a, lows_a, highs_b, lows_b, inverses, whole_b)
        carry_a = small(carry_kernel, block, other_step, other_a, met_a, token)
        leaf_share, token = leaf_values(tiles, ((0, True),), columns, gains, [solved_a], [carry_a], ())
        carry_b = small(carry_kernel, block, other_step, other_b, met_b, token)
    else:
        solved_a, solved_b, gains, _ = freed(highs_a, lows_a, highs_b, lows_b, inverses, mapped)
        carry = scanned(section, jnp.concatenate([offset_a, offset_b, step], 1), 2 * LANES)
        carry_a, carry_b = carry[:, :LANES], carry[:, LANES:]
        leaf_share, _ = leaf_values(tiles, ((0, True),), columns, gains, [solved_a], [carry_a], ())
    theirs_a = swapped(carry_a, "tile", 1)
    theirs_b = swapped(carry_b, "tile", 1)
    shared = (step, offset_a, carry_a, offset_b, carry_b) if tiles == 4 else ()
    middle = leaf_values(tiles, ((0, False), (1, True)), columns, gains, [solved_a, solved_b], [theirs_a, carry_b], shared, leaf_share)
    (leaf_share,) = leaf_values(tiles, ((1, False),), columns, gains, [solved_b], [theirs_b], (), middle[0])
    if tiles == 4:
        sep_share = middle[1]
    else:
        own = affine(step, jnp.concatenate([carry_a, carry_b], 1), jnp.concatenate([offset_a, offset_b], 1))
        others = swapped(own, "tile", 1)
        lower = jnp.where(tile % 2 == 0, own, others)
        upper = jnp.where(tile % 2 == 0, others, own)
        sep_share = lax.dynamic_slice_in_dim(jnp.concatenate([lower, upper], 1), tile * width, width, 1)
    return (leaf_share[None], sep_share[None])


def solution(mesh):
    return jax.shard_map(
        shards,
        mesh=mesh,
        in_specs=(
            P(("parts", "chain"), "tile", None, None),
            P(("parts", "chain"), "tile", None, None),
            P(("parts", "chain"), "tile", None, None),
            P(("parts", "chain"), "tile", None, None),
            P(("parts", "chain"), "tile"),
            P(("parts", "chain"), None, None),
            P(("parts", "chain"), None, None),
            P(("parts", "chain"), None, None),
        ),
        out_specs=(P(("parts", "chain"), "tile", None, None), P(("parts", "chain"), None, "tile")),
        check_vma=False,
    )
```
